256 devices in a mesh: dp: 8 (over x, z_hi), tensor: 8 (over y, core), expert: 4 (over z_lo).
Axes of the slice: x: 4, y: 4, z: 8 (z_hi: 2, z_lo: 4; z = z_hi * 4 + z_lo), core: 2. Of those that a mesh axis runs over, the one named last changes fastest.
Arguments:
- moe_input: bfloat16 [8192, 2048], P(('dp', 'tensor'), 'expert'), may hold values from -6 to 6
- grad_output: bfloat16 [8192, 2048], P(('dp', 'tensor'), 'expert'), may hold values from -6 to 6
- routes: int32 [8192, 8], P(('dp', 'tensor')), may hold values from 0 to 127, all different within a row; in each aligned block of 128 rows (0 to 127, 128 to 255, ...) at most 12 rows name the same one
- route_weight: float32 [8192, 8], P(('dp', 'tensor')), may hold values from 0.05 to 0.35
- capacity: int32 [128], replicated, may hold values from 6 to 12, as said below
- w_gate: bfloat16 [256, 384, 2048], P(('dp', 'tensor', 'expert')), may hold values from -0.125 to 0.125
- w_up: bfloat16 [256, 384, 2048], P(('dp', 'tensor', 'expert')), may hold values from -0.125 to 0.125
- w_down: bfloat16 [256, 384, 2048], P(('dp', 'tensor', 'expert')), may hold values from -0.21875 to 0.21875
Outputs:
- moe_output: bfloat16 [8192, 2048], P(('dp', 'tensor'), 'expert')
- grad_input: bfloat16 [8192, 2048], P(('dp', 'tensor'), 'expert')
- grad_gate: bfloat16 [256, 384, 2048], P(('dp', 'tensor', 'expert'))
- grad_up: bfloat16 [256, 384, 2048], P(('dp', 'tensor', 'expert'))
- grad_down: bfloat16 [256, 384, 2048], P(('dp', 'tensor', 'expert'))
The draws below stay inside these ranges and needn't reach their ends.
Inputs may be any that keep to these rules, and one draw needn't show every extreme that they name: `routes`: each row names 8 different experts; within each aligned block of 128 rows (the rows of one device) no expert is named more than 12 times. Some expert has a capacity of exactly 12.
All inputs are finite; a program needn't handle non-finite values.
Results may differ from the reference program's by a relative error of at most 0.0071.
Values may be sent and summed in bfloat16 or wider, within the bound.
A program may use at most 128 MiB of HBM per device.

```python
import math
import jax
import jax.numpy as jnp
import numpy as np
from jax import lax

D = 2048
HID = 768
TOPK = 8
TOK_DEV = 128
EXPERTS = 128
MOST = 12
TOKENS = 8192
N_DP = 8
N_TENSOR = 8


def draw_capacity(key, part):
    inner = jax.random.fold_in(key, 17)
    key_caps, key_pick = jax.random.split(inner)
    base_caps = jax.random.randint(key_caps, (EXPERTS,), (MOST + 1) // 2, MOST + 1)
    chosen = jax.random.randint(key_pick, (), 0, EXPERTS)
    return jnp.where(jnp.arange(EXPERTS) == chosen, MOST, base_caps).astype(jnp.int32)


def level_of(own_key, dims, shards, low, largest):
    def one(position, parts):
        draws = jax.random.uniform(jax.random.fold_in(jax.random.fold_in(own_key, 6), position), (parts,), jnp.float32, low / len(shards), largest / len(shards))
        return jnp.repeat(jnp.exp(draws), dims[position] // parts).reshape((-1,) + (1,) * (len(dims) - position - 1))

    factor_of = one(*shards[0])
    for cut in shards[1:]:
        factor_of = factor_of * one(*cut)
    return factor_of


def assign_block(rng, own, number, rows, number_of, top, bound, lean):
    sequence = jax.random.permutation(rng, number_of)
    packed, ordinary = portions_of(number_of, rows * top, bound, lean, True), portions_of(number_of, rows * top, bound, lean, False)
    places = jnp.arange(number_of)

    def named(lengths, rotation):
        used = int((lengths > 0).sum())
        fixed = max(1, used // 4)
        shifted = fixed + (places - fixed + rotation * (used - fixed)) % max(1, number_of - fixed)
        return jnp.zeros((number_of,), jnp.int32).at[sequence[jnp.where(places < fixed, places, shifted)]].set(jnp.asarray(lengths, jnp.int32))

    lengths = jnp.where(number % 4 == 0, named(packed, number // 4), named(ordinary, number - number // 4 - 1))
    mixed = jax.random.permutation(jax.random.fold_in(own, 3), number_of)
    donor, receiver = mixed[0:number_of // 2 * 2:2], mixed[1:number_of // 2 * 2:2]
    room = jnp.minimum(lengths[donor] - 1, bound - lengths[receiver]) // 2
    room = jnp.where((donor == sequence[0]) | (receiver == sequence[0]) | (lengths[receiver] == 0), 0, jnp.maximum(room, 0))
    shifted = jax.random.randint(jax.random.fold_in(own, 4), (number_of // 2,), 0, 1 << 20) % (room + 1)
    lengths = lengths.at[donor].add(-shifted).at[receiver].add(shifted)
    members = jnp.searchsorted(jnp.cumsum(lengths), jnp.arange(rows * top), side="right").astype(jnp.int32)
    table = members.reshape(top, rows).T
    table = table[jax.random.permutation(jax.random.fold_in(own, 1), rows)]
    rotation = jax.random.randint(jax.random.fold_in(own, 2), (rows, 1), 0, top)
    return jnp.take_along_axis(table, (jnp.arange(top)[None, :] + rotation) % top, axis=1)


def portions_of(count, total, bound, lean, full):
    loads = [(1 << 20) // math.isqrt(rank ** lean) + 1 for rank in range(1, count + 1)]
    largest = bound if full else min(bound, max(-(-total // count), total * loads[0] // sum(loads)))
    least = 1 if total - largest >= count - 1 else 0
    holding, spare = [largest] + [least] * (count - 1), total - largest - least * (count - 1)
    while spare > 0:
        candidates = [i for i in range(1, count) if holding[i] < largest] or [i for i in range(1, count) if holding[i] < bound]
        whole, left = sum([loads[i] for i in candidates]), spare
        for i in candidates:
            extra = min(bound - holding[i], max(1, left * loads[i] // whole), spare)
            holding[i] = holding[i] + extra
            spare = spare - extra
    return np.array(holding)


def noise(own_key, extent, width, reach, shards=(), kind=jnp.bfloat16):
    values = jax.random.normal(own_key, extent, jnp.float32) * width
    if len(shards) > 0:
        values = level_of(own_key, extent, shards, -0.22, 0.18) * values
    return jnp.clip(values, min=-reach, max=reach).astype(kind)


def setup_inputs(seed: int = 0) -> dict:
    seeds = jax.random.split(jax.random.key(seed), 9)
    moe_input = noise(seeds[0], (TOKENS, D), 1.0, 6.0, ((0, 64), (1, 4)))
    grad_output = noise(seeds[1], (TOKENS, D), 1.0, 6.0, ((0, 64), (1, 4)))
    routes_keys = jax.random.split(jax.random.fold_in(seeds[2], 1), TOKENS // TOK_DEV)
    routes_turns = jax.random.permutation(jax.random.fold_in(seeds[2], 3), TOKENS // TOK_DEV)
    routes = jax.vmap(lambda own, number: assign_block(jax.random.fold_in(seeds[2], 2), own, number, TOK_DEV, EXPERTS, TOPK, MOST, 2))(routes_keys, routes_turns).reshape((TOKENS, TOPK))
    route_weight = jnp.clip(0.05 + 0.29999999 * jax.random.uniform(seeds[3], (TOKENS, TOPK), jnp.float32) ** level_of(seeds[3], (TOKENS, TOPK), ((0, 64),), -0.2, 0.2), 0.05, 0.35)
    capacity = draw_capacity(jax.random.fold_in(seeds[8], 71), 0)
    w_gate = noise(seeds[5], (2 * EXPERTS, HID // 2, D), D ** -0.5, 0.125, ((0, 256),))
    w_up = noise(seeds[6], (2 * EXPERTS, HID // 2, D), D ** -0.5, 0.125, ((0, 256),))
    w_down = noise(seeds[7], (2 * EXPERTS, HID // 2, D), HID ** -0.5, 0.21875, ((0, 256),))
    return {"moe_input": moe_input, "grad_output": grad_output, "routes": routes, "route_weight": route_weight, "capacity": capacity, "w_gate": w_gate, "w_up": w_up, "w_down": w_down}


def place_block(flat_routes, capacity):
    onehot = (flat_routes[:, None] == jnp.arange(EXPERTS, dtype=jnp.int32)[None, :]).astype(jnp.int32)
    before = jnp.cumsum(onehot, axis=0) - onehot
    pair_rank = jnp.sum(onehot * before, axis=1)
    pair_limit = jnp.sum(onehot * capacity[None, :], axis=1)
    pair_place = jnp.where(pair_rank < pair_limit, flat_routes * MOST + pair_rank, EXPERTS * MOST)
    return pair_place.astype(jnp.int32)


def spread_ints(pair_place, values):
    return jnp.full((EXPERTS * MOST + 1,), TOKENS, jnp.int32).at[pair_place].set(values)[:EXPERTS * MOST]


def spread_floats(pair_place, values):
    return jnp.zeros((EXPERTS * MOST + 1,), jnp.float32).at[pair_place].set(values)[:EXPERTS * MOST]


def reference(moe_input, grad_output, routes, route_weight, capacity, w_gate, w_up, w_down):
    groups = N_DP * N_TENSOR
    pair_count = TOK_DEV * TOPK
    half = HID // 2
    gate_all = w_gate.reshape(EXPERTS, HID, D)
    up_all = w_up.reshape(EXPERTS, HID, D)
    down_all = w_down.reshape(EXPERTS, HID, D)
    places = jax.vmap(place_block, in_axes=(0, None))(routes.reshape(groups, pair_count), capacity)
    pair_token = jnp.arange(pair_count, dtype=jnp.int32) // TOPK
    token_ids = pair_token[None, :] + (jnp.arange(groups, dtype=jnp.int32) * TOK_DEV)[:, None]
    slot_owner = jax.vmap(spread_ints)(places, token_ids)
    slot_weight = jax.vmap(spread_floats)(places, route_weight.reshape(groups, pair_count).astype(jnp.float32))
    owner_rows = slot_owner.reshape(groups, EXPERTS, MOST).transpose(1, 0, 2).reshape(EXPERTS, groups * MOST)
    weight_rows = slot_weight.reshape(groups, EXPERTS, MOST).transpose(1, 0, 2).reshape(EXPERTS, groups * MOST)
    padded_input = jnp.concatenate([moe_input, jnp.zeros((1, D), moe_input.dtype)], axis=0)
    padded_cot = jnp.concatenate([grad_output, jnp.zeros((1, D), grad_output.dtype)], axis=0)

    def expert_step(running, operands):
        slot_ids, weights, gate_w, up_w, down_w = operands
        slot_rows = padded_input[slot_ids]
        slot_cots = (weights[:, None] * padded_cot[slot_ids].astype(jnp.float32)).astype(jnp.bfloat16)
        gate_pre = jnp.dot(slot_rows, gate_w.T, preferred_element_type=jnp.float32)
        up_pre = jnp.dot(slot_rows, up_w.T, preferred_element_type=jnp.float32)
        sigmoid_gate = jax.nn.sigmoid(gate_pre)
        gate_act = gate_pre * sigmoid_gate
        hidden = (gate_act * up_pre).astype(jnp.bfloat16)
        hidden_cot = jnp.dot(slot_cots, down_w.T, preferred_element_type=jnp.float32)
        gate_cot = (hidden_cot * up_pre * sigmoid_gate * (1.0 + gate_pre * (1.0 - sigmoid_gate))).astype(jnp.bfloat16)
        up_cot = (hidden_cot * gate_act).astype(jnp.bfloat16)
        out_total = jnp.zeros((slot_rows.shape[0], D), jnp.float32)
        in_total = jnp.zeros((slot_rows.shape[0], D), jnp.float32)
        for part_index in range(2):
            low = part_index * half
            high = low + half
            out_part = lax.optimization_barrier(jnp.dot(hidden[:, low:high], down_w[low:high], preferred_element_type=jnp.float32).astype(jnp.bfloat16))
            in_sum = jnp.dot(gate_cot[:, low:high], gate_w[low:high], preferred_element_type=jnp.float32)
            in_sum = in_sum + jnp.dot(up_cot[:, low:high], up_w[low:high], preferred_element_type=jnp.float32)
            in_part = lax.optimization_barrier(in_sum.astype(jnp.bfloat16))
            out_total = out_total + out_part.astype(jnp.float32)
            in_total = in_total + in_part.astype(jnp.float32)
        expert_out = out_total.astype(jnp.bfloat16)
        input_slot = in_total.astype(jnp.bfloat16)
        out_acc, in_acc = running
        out_acc = out_acc.at[slot_ids].add(weights[:, None] * expert_out.astype(jnp.float32))
        in_acc = in_acc.at[slot_ids].add(input_slot.astype(jnp.float32))
        grad_gate = jnp.dot(gate_cot.T, slot_rows, preferred_element_type=jnp.float32).astype(jnp.bfloat16)
        grad_up = jnp.dot(up_cot.T, slot_rows, preferred_element_type=jnp.float32).astype(jnp.bfloat16)
        grad_down = jnp.dot(hidden.T, slot_cots, preferred_element_type=jnp.float32).astype(jnp.bfloat16)
        return (out_acc, in_acc), (grad_gate, grad_up, grad_down)

    start = (jnp.zeros((TOKENS + 1, D), jnp.float32), jnp.zeros((TOKENS + 1, D), jnp.float32))
    finals, grads = lax.scan(expert_step, start, (owner_rows, weight_rows, gate_all, up_all, down_all))
    out_acc, in_acc = finals
    grad_gate = grads[0].reshape(2 * EXPERTS, half, D)
    grad_up = grads[1].reshape(2 * EXPERTS, half, D)
    grad_down = grads[2].reshape(2 * EXPERTS, half, D)
    return out_acc[:TOKENS].astype(jnp.bfloat16), in_acc[:TOKENS].astype(jnp.bfloat16), grad_gate, grad_up, grad_down
```

```python
import functools
import jax
import jax.numpy as jnp
from jax import lax
from jax.experimental import pallas as pl
from jax.experimental.pallas import tpu as pltpu
from jax.sharding import PartitionSpec as P

MESH = pl.DeviceIdType.MESH
F32 = jnp.float32
BF16 = jnp.bfloat16
PLANE = ((1, 0), (0, 1), (3, 0), (0, 3), (1, 1), (3, 3), (1, 3), (3, 1), (2, 0), (0, 2), (2, 1), (1, 2), (2, 3), (3, 2), (2, 2))
PLANE_X = sum(o[0] * 4**i for i, o in enumerate(PLANE))
PLANE_Y = sum(o[1] * 4**i for i, o in enumerate(PLANE))
OTHERS = tuple((dx, dy, 0, 0) for dx, dy in PLANE) + (
    (0, 0, 1, 0), (0, 0, 7, 0), (0, 0, 0, 1), (0, 0, 4, 0), (0, 0, 4, 1))


def device(x, y, z, c):
    return ((x % 4) * 2 + (z % 8) // 4, (y % 4) * 2 + c % 2, z % 4)


def nn(a, b):
    return jnp.dot(a, b, preferred_element_type=F32)


def nt(a, b):
    return lax.dot_general(a, b, (((1,), (1,)), ((), ())), preferred_element_type=F32)


def tiles(count, body):
    def step(i, carry):
        body(i)
        return carry

    lax.fori_loop(0, count, step, 0)


def rows_of(i, size):
    return pl.ds(pl.multiple_of(i * size, size), size)


def kernel(tok_ref, cot_ref, meta_ref, ids_ref, wg, wu, wd,
           out_ref, gin_ref, gg, gu, gd,
           X, S, R, B, W, G, pre, hc, hid, cot2, cT, hT, Pm, Wf, PT, Wh, Wl, wsl, meta, FA, CS, CR, QS, QR,
           w_sem, g_sem, m_ssem, m_rsem, a_ssem, a_rsem, ac_ssem, ac_rsem, d_ssem, d_rsem, o_ssem, o_rsem,
           c_ssem, c_rsem, q_ssem, q_rsem):
    dp, tn, ex = lax.axis_index("dp"), lax.axis_index("tensor"), lax.axis_index("expert")
    x, y, z, c = dp // 2, tn // 2, (dp % 2) * 4 + ex, tn % 2
    me = x * 4 + y
    late = []

    def remote(src, dst, ssem, rsem, to):
        return pltpu.make_async_remote_copy(
            src_ref=src, dst_ref=dst, send_sem=ssem, recv_sem=rsem, device_id=to, device_id_type=MESH)

    barrier = pltpu.get_barrier_semaphore()
    for dx, dy, dz, dc in OTHERS:
        pl.semaphore_signal(barrier, inc=1, device_id=device(x + dx, y + dy, z + dz, c + dc), device_id_type=MESH)

    loads = []
    for q in range(4):
        for j, w in enumerate((wg, wu, wd)):
            cp = pltpu.make_async_copy(w.at[0, :, pl.ds(q * 512, 512)], W.at[q, pl.ds(j * 384, 384)], w_sem.at[q, j])
            cp.start()
            loads.append(cp)

    zq, zh = z % 4, z // 4
    X[0, c, zq, zh] = tok_ref[...]
    X[1, c, zq, zh] = cot_ref[...]
    own = c * 2 + zh
    meta[own] = meta_ref[...]
    pl.semaphore_wait(barrier, len(OTHERS))

    notes = []
    for i, (dz, dc) in enumerate(((0, 1), (4, 0), (4, 1))):
        cp = remote(meta.at[own], meta.at[own], m_ssem.at[i], m_rsem.at[i], device(x, y, z + dz, c + dc))
        cp.start()
        notes.append(cp)

    def piece(arr, pz, half=None, core=None):
        pz = (pz + 8) % 8
        ref = X.at[arr, c if core is None else core, pz % 4, pz // 4]
        return ref if half is None else ref.at[pl.ds(half * 64, 64)]

    def ring_send(arr, s):
        for d, sgn in enumerate((1, -1)):
            src = piece(arr, z - sgn * s, d if s == 3 else None)
            cp = remote(src, src, a_ssem.at[arr, d, s], a_rsem.at[arr, d, s], device(x, y, z + sgn + 8, c))
            cp.start()
            late.append(cp)

    def ring_wait(arr, s):
        for d, sgn in enumerate((1, -1)):
            dst = piece(arr, z - sgn * (s + 1), d if s == 3 else None)
            remote(dst, dst, a_ssem.at[arr, d, s], a_rsem.at[arr, d, s], device(x, y, z + sgn + 8, c)).wait_recv()

    def core_send(arr, off):
        src = piece(arr, z + off)
        cp = remote(src, src, ac_ssem.at[arr, off + 3], ac_rsem.at[arr, off + 3], device(x, y, z, c + 1))
        cp.start()
        late.append(cp)

    def core_wait(arr, off):
        dst = piece(arr, z + off, core=1 - c)
        remote(dst, dst, ac_ssem.at[arr, off + 3], ac_rsem.at[arr, off + 3], device(x, y, z, c + 1)).wait_recv()

    def spread(src, dst, ssem, rsem, arr, q):
        mine = pl.ds(pl.multiple_of(me * 48, 48), 48)
        dst[arr, q, mine] = src[arr, q, mine]

        def one(i, carry):
            tx, ty = carry
            px, py = (x + tx % 4) % 4, (y + ty % 4) % 4
            there = pl.ds(pl.multiple_of((px * 4 + py) * 48, 48), 48)
            remote(src.at[arr, q, there], dst.at[arr, q, mine], ssem.at[arr, q], rsem.at[arr, q],
                   device(px, py, z, c)).start()
            return tx // 4, ty // 4

        lax.fori_loop(0, 15, one, (jnp.int32(PLANE_X), jnp.int32(PLANE_Y)))

    def all_of(ref, sem, arr, q):
        part = ref.at[arr, q, pl.ds(0, 720)]
        pltpu.make_async_copy(part, part, sem.at[arr, q]).wait()

    def select(arr, rel):
        q = (z + rel) % 4
        for off in {2: (2, -2), 1: (1, -3), 3: (-1, 3), 0: (0, 4)}[rel]:
            core_wait(arr, off)

        def body(i):
            m = rows_of(i, 256)
            v = nn(Pm[m, 0:256], X[arr, 0, q].reshape(256, 512)) + nn(Pm[m, 256:512], X[arr, 1, q].reshape(256, 512))
            if arr == 1:
                v = v * wsl[m, 0:1]
            S[arr, q, m] = v.astype(BF16)

        tiles(3, body)
        spread(S, R, d_ssem, d_rsem, arr, q)

    ring_send(0, 0)
    core_send(0, 0)
    for cp in notes:
        cp.wait()

    upper = (lax.broadcasted_iota(jnp.int32, (128, 128), 0) < lax.broadcasted_iota(jnp.int32, (128, 128), 1))
    upper = upper.astype(F32).astype(BF16)

    def build(i):
        m = rows_of(i, 256)
        rank = ids_ref[m, 4:5]
        total = jnp.zeros((256, 1), F32)
        for b in range(4):
            want = ids_ref[m, b:b + 1]
            hit = jnp.zeros((256, 128), F32)
            weight = jnp.zeros((256, 128), F32)
            for k in range(8):
                same = want == meta[b, k:k + 1, :]
                hit = jnp.where(same, 1.0, hit)
                weight = jnp.where(same, meta[b, k + 8:k + 9, :], weight)
            before = nn(hit.astype(BF16), upper)
            chosen = before == rank
            hit = jnp.where(chosen, hit, 0.0)
            weight = jnp.where(chosen, weight, 0.0)
            Pm[m, b * 128:(b + 1) * 128] = hit.astype(BF16)
            Wf[m, b * 128:(b + 1) * 128] = weight
            total = total + jnp.sum(weight, axis=1, keepdims=True)
        wsl[m] = jnp.broadcast_to(total, (256, 128))

    tiles(3, build)

    for arr in (0, 1):
        ring_wait(arr, 0)
        ring_send(arr, 1)
        core_send(arr, 1)
        core_send(arr, -1)
        ring_wait(arr, 1)
        ring_send(arr, 2)
        core_send(arr, 2)
        core_send(arr, -2)
        select(arr, 2)
        ring_wait(arr, 2)
        ring_send(arr, 3)
        core_send(arr, 3)
        core_send(arr, -3)
        if arr == 0:
            ring_send(1, 0)
            core_send(1, 0)
        select(arr, 1)
        select(arr, 3)
        ring_wait(arr, 3)
        core_send(arr, 4)
        select(arr, 0)

    for cp in loads:
        cp.wait()

    for k, rel in enumerate((2, 1, 3, 0)):
        q = (z + rel) % 4
        all_of(R, d_rsem, 0, q)

        def body(i, k=k, q=q):
            m = rows_of(i, 256)
            v = nt(R[0, q, m], W[q, 0:768])
            pre[m] = v if k == 0 else pre[m] + v

        tiles(3, body)

    def act(i):
        m = rows_of(i, 128)
        g, u = pre[m, 0:384], pre[m, 384:768]
        hid[m] = (g * jax.nn.sigmoid(g) * u).astype(BF16)

    tiles(6, act)

    for rel in (0, 1, 3, 2):
        q = (z + rel) % 4
        all_of(S, d_ssem, 0, q)

        def body(i, q=q):
            m = rows_of(i, 256)
            S[0, q, m] = nn(hid[m], W[q, 768:1152]).astype(BF16)

        tiles(3, body)
        spread(S, B, o_ssem, o_rsem, 0, q)

    def turn(i):
        m = rows_of(i, 256)
        for b in range(4):
            t = pl.ds(b * 128, 128)
            weight = Wf[m, b * 128:(b + 1) * 128].T
            high = weight.astype(BF16)
            Wh[t, m] = high
            Wl[t, m] = (weight - high.astype(F32)).astype(BF16)
            PT[t, m] = Pm[m, b * 128:(b + 1) * 128].astype(F32).T.astype(BF16)

    tiles(3, turn)

    for k, rel in enumerate((2, 1, 3, 0)):
        q = (z + rel) % 4
        all_of(R, d_rsem, 1, q)

        def body(i, k=k, q=q):
            m = rows_of(i, 256)
            v = nt(R[1, q, m], W[q, 768:1152])
            hc[m] = v if k == 0 else hc[m] + v

        tiles(3, body)

    def cots(i):
        m = rows_of(i, 128)
        g, u, h = pre[m, 0:384], pre[m, 384:768], hc[m]
        s = jax.nn.sigmoid(g)
        cot2[m, 0:384] = (h * u * s * (1.0 + g * (1.0 - s))).astype(BF16)
        cot2[m, 384:768] = (h * (g * s)).astype(BF16)

    tiles(6, cots)

    for rel in (0, 1, 3, 2):
        q = (z + rel) % 4
        all_of(S, d_ssem, 1, q)

        def body(i, q=q):
            m = rows_of(i, 256)
            S[1, q, m] = nn(cot2[m], W[q, 0:768]).astype(BF16)

        tiles(3, body)
        spread(S, B, o_ssem, o_rsem, 1, q)

    def turn2(i):
        m = rows_of(i, 128)
        cT[:, m] = cot2[m].astype(F32).T.astype(BF16)
        hT[:, m] = hid[m].astype(F32).T.astype(BF16)

    tiles(6, turn2)
    stores = []
    for q in range(4):
        def body(i, q=q):
            m = rows_of(i, 256)
            G[q, m] = nn(cT[m], R[0, q]).astype(BF16)

        tiles(3, body)
        G[q, 768:1152] = nn(hT[...], R[1, q]).astype(BF16)
        for j, o in enumerate((gg, gu, gd)):
            cp = pltpu.make_async_copy(G.at[q, pl.ds(j * 384, 384)], o.at[0, :, pl.ds(q * 512, 512)], g_sem.at[q, j])
            cp.start()
            stores.append(cp)

    def process(arr, rel):
        q = (z + rel) % 4
        all_of(B, o_rsem, arr, q)

        def summed(core):
            t = rows_of(core, 256)
            if arr == 0:
                return nn(Wh[t], B[0, q]) + nn(Wl[t], B[0, q])
            return nn(PT[t], B[1, q])

        CS[arr, q] = summed(1 - c).astype(BF16)
        cp = remote(CS.at[arr, q], CR.at[arr, q], c_ssem.at[arr, q], c_rsem.at[arr, q], device(x, y, z, c + 1))
        cp.start()
        late.append(cp)
        FA[arr, q] = summed(c)
        return cp

    def total(arr, d, low=0, size=128):
        d = (d + 8) % 8
        t = pl.ds(pl.multiple_of((d // 4) * 128 + low, 64), size)
        return FA[arr, d % 4, t] + CR[arr, d % 4, t].astype(F32)

    def back_send(arr, s):
        for d, sgn in enumerate((1, -1)):
            dest = z + sgn * (4 - s)
            if s == 0:
                QS[arr, d, 0, d * 64:d * 64 + 64] = total(arr, dest, d * 64, 64).astype(BF16)
                src, dst = QS.at[arr, d, 0, pl.ds(d * 64, 64)], QR.at[arr, d, 0, pl.ds(d * 64, 64)]
            else:
                back_wait(arr, d, s - 1)
                if s == 1:
                    h = slice(d * 64, d * 64 + 64)
                    o = (1 - d) * 64
                    QS[arr, d, 1, h] = (total(arr, dest, d * 64, 64) + QR[arr, d, 0, h].astype(F32)).astype(BF16)
                    QS[arr, d, 1, o:o + 64] = total(arr, dest, o, 64).astype(BF16)
                else:
                    QS[arr, d, s] = (total(arr, dest) + QR[arr, d, s - 1].astype(F32)).astype(BF16)
                src, dst = QS.at[arr, d, s], QR.at[arr, d, s]
            cp = remote(src, dst, q_ssem.at[arr, d, s], q_rsem.at[arr, d, s], device(x, y, z + sgn + 8, c))
            cp.start()
            late.append(cp)

    def back_wait(arr, d, s):
        dst = QR.at[arr, d, s, pl.ds(d * 64, 64)] if s == 0 else QR.at[arr, d, s]
        remote(dst, dst, q_ssem.at[arr, d, s], q_rsem.at[arr, d, s], device(x, y, z + 1, c)).wait_recv()

    for arr, o_ref in ((0, out_ref), (1, gin_ref)):
        process(arr, 0).wait_recv()
        back_send(arr, 0)
        first = process(arr, 1)
        process(arr, 3).wait_recv()
        first.wait_recv()
        back_send(arr, 1)
        process(arr, 2).wait_recv()
        back_send(arr, 2)
        back_send(arr, 3)
        back_wait(arr, 0, 3)
        back_wait(arr, 1, 3)
        o_ref[...] = (total(arr, z) + QR[arr, 0, 3].astype(F32) + QR[arr, 1, 3].astype(F32)).astype(BF16)

    for arr in (0, 1):
        for q in range(4):
            all_of(S, o_ssem, arr, q)
    for cp in late:
        cp.wait_send()
    for cp in stores:
        cp.wait()


def shards(moe_input, grad_output, routes, route_weight, capacity, w_gate, w_up, w_down):
    dp, tn, ex = lax.axis_index("dp"), lax.axis_index("tensor"), lax.axis_index("expert")
    meta = jnp.concatenate([routes.astype(F32).T, route_weight.T], axis=0)
    row = jnp.arange(768, dtype=jnp.int32)
    chip, block, rank = row // 48, row % 48 // 12, row % 12
    group = ((chip // 4) * 2 + dp % 2) * 8 + (chip % 4) * 2 + tn % 2
    expert = 2 * group + ex // 2
    open_slot = rank < capacity[expert]
    lane = jnp.arange(8, dtype=jnp.int32)[None, :]
    ids = jnp.where((lane == block[:, None]) & open_slot[:, None], expert[:, None], -1)
    ids = jnp.where(lane == 4, rank[:, None], ids).astype(F32)
    vmem = pl.BlockSpec(memory_space=pltpu.VMEM)
    hbm = pl.BlockSpec(memory_space=pl.ANY)
    dma = pltpu.SemaphoreType.DMA
    grad = jax.ShapeDtypeStruct((1, 384, 2048), BF16)
    tok = jax.ShapeDtypeStruct((128, 512), BF16)
    big = pltpu.VMEM((2, 4, 768, 512), BF16)
    return pl.pallas_call(
        kernel,
        out_shape=(tok, tok, grad, grad, grad),
        in_specs=[vmem] * 4 + [hbm] * 3,
        out_specs=(vmem, vmem, hbm, hbm, hbm),
        scratch_shapes=[
            pltpu.VMEM((2, 2, 4, 2, 128, 512), BF16),
            big, big, big,
            pltpu.VMEM((4, 1152, 512), BF16),
            pltpu.VMEM((4, 1152, 512), BF16),
            pltpu.VMEM((768, 768), F32),
            pltpu.VMEM((768, 384), F32),
            pltpu.VMEM((768, 384), BF16),
            pltpu.VMEM((768, 768), BF16),
            pltpu.VMEM((768, 768), BF16),
            pltpu.VMEM((384, 768), BF16),
            pltpu.VMEM((768, 512), BF16),
            pltpu.VMEM((768, 512), F32),
            pltpu.VMEM((512, 768), BF16),
            pltpu.VMEM((512, 768), BF16),
            pltpu.VMEM((512, 768), BF16),
            pltpu.VMEM((768, 128), F32),
            pltpu.VMEM((4, 16, 128), F32),
            pltpu.VMEM((2, 4, 256, 512), F32),
            pltpu.VMEM((2, 4, 256, 512), BF16),
            pltpu.VMEM((2, 4, 256, 512), BF16),
            pltpu.VMEM((2, 2, 4, 128, 512), BF16),
            pltpu.VMEM((2, 2, 4, 128, 512), BF16),
            dma((4, 3)), dma((4, 3)), dma((3,)), dma((3,)),
            dma((2, 2, 4)), dma((2, 2, 4)), dma((2, 8)), dma((2, 8)),
            dma((2, 4)), dma((2, 4)), dma((2, 4)), dma((2, 4)),
            dma((2, 4)), dma((2, 4)), dma((2, 2, 4)), dma((2, 2, 4)),
        ],
        compiler_params=pltpu.CompilerParams(
            collective_id=0, has_side_effects=True, vmem_limit_bytes=60 * 2**20),
        cost_estimate=pl.CostEstimate(flops=11 * 10**9, bytes_accessed=10**7, transcendentals=10**6),
        name="moe_step",
    )(moe_input, grad_output, meta, ids, w_gate, w_up, w_down)


def solution(mesh):
    tok = P(("dp", "tensor"), "expert")
    row = P(("dp", "tensor"), None)
    weight = P(("dp", "tensor", "expert"), None, None)
    return jax.shard_map(
        shards, mesh=mesh, in_specs=(tok, tok, row, row, P(), weight, weight, weight),
        out_specs=(tok, tok, weight, weight, weight), check_vma=False)
```
